512 devices in a mesh: outer: 32 (over y, x, core), inner: 16 (over z).
Axes of the slice: x: 4, y: 4, z: 16, core: 2. Of those that a mesh axis runs over, the one named last changes fastest.
Arguments:
- queries: bfloat16 [65536, 2048], P(('outer', 'inner')), may hold values from -6 to 6
- keys: bfloat16 [65536, 2048], P(('outer', 'inner')), may hold values from -6 to 6
- values: bfloat16 [65536, 2048], P(('outer', 'inner')), may hold values from -7 to 7
- cotangent: bfloat16 [65536, 2048], P(('outer', 'inner')), may hold values from -7 to 7
Outputs:
- attended: bfloat16 [65536, 2048], P(('outer', 'inner'))
- query_grad: bfloat16 [65536, 2048], P(('outer', 'inner'))
- key_grad: bfloat16 [65536, 2048], P(('outer', 'inner'))
- value_grad: bfloat16 [65536, 2048], P(('outer', 'inner'))
The draws below stay inside these ranges and needn't reach their ends.
All inputs are finite; a program needn't handle non-finite values.
Results may differ from the reference program's by a relative error of at most 0.013.
The reference program's roundings to bfloat16 on the way (of `q_feat`, `k_feat`, `weights`, `state_low`, `grad_scaled`, `grad_scores` and `later_low`) count: a program that leaves them out, or rounds other values in their place, can miss the bound.
Values sent between devices are 32-bit elements; how exact they have to be, the bound alone decides.
A program may use at most 128 MiB of HBM per device.

```python
import jax
import jax.numpy as jnp
from jax import lax

HEADS = 16
HD = 128
TOK_DEV = 128
TOKENS = 65536


def shifted_normal(key, salt):
    key = jax.random.fold_in(key, salt)
    first, second = jax.random.split(key)
    blocks = TOKENS // TOK_DEV
    offset = jnp.clip(jax.random.normal(first, (blocks, 1, HEADS * HD), jnp.float32), -3.0, 3.0)
    noise = jnp.clip(jax.random.normal(second, (blocks, TOK_DEV, HEADS * HD), jnp.float32), -4.0, 4.0)
    return (offset + noise).reshape(TOKENS, HEADS * HD)


def draw_values(key, part):
    return shifted_normal(key, 11).astype(jnp.bfloat16)


def draw_cotangent(key, part):
    return shifted_normal(key, 23).astype(jnp.bfloat16)


def shard_levels(key, dims, cuts, smallest, largest):
    gain, own = 1.0, jax.random.fold_in(key, 6)
    for dim, blocks in cuts:
        draws = jnp.exp(jax.random.uniform(jax.random.fold_in(own, dim), (blocks,), jnp.float32, smallest / len(cuts), largest / len(cuts)))
        gain = gain * jnp.repeat(draws, dims[dim] // blocks).reshape([-1 if axis == dim else 1 for axis in range(len(dims))])
    return gain


def gaussian(stream_key, dims, scale, limit, cuts=(), kind=jnp.bfloat16):
    level = shard_levels(stream_key, dims, cuts, -0.22, 0.18) if cuts else 1.0
    entries = jax.random.normal(stream_key, dims, jnp.float32) * scale * level
    return jnp.minimum(jnp.maximum(entries, -limit), limit).astype(kind)


def setup_inputs(seed: int = 0) -> dict:
    key_of = jax.random.split(jax.random.key(seed), 5)
    queries = gaussian(key_of[0], (TOKENS, HEADS * HD), 1.0, 6.0, ((0, 512),))
    keys = gaussian(key_of[1], (TOKENS, HEADS * HD), 1.0, 6.0, ((0, 512),))
    values = draw_values(jax.random.fold_in(key_of[4], 71), 0)
    cotangent = draw_cotangent(jax.random.fold_in(key_of[4], 71), 0)
    return dict(queries=queries, keys=keys, values=values, cotangent=cotangent)


def features(x):
    wide = x.astype(jnp.float32)
    return jnp.where(wide > 0, wide + 1.0, jnp.exp(jnp.minimum(wide, 0.0)))


def slope(x):
    wide = x.astype(jnp.float32)
    return jnp.where(wide > 0, 1.0, jnp.exp(jnp.minimum(wide, 0.0)))


def reference(queries, keys, values, cotangent):
    blocks = TOKENS // TOK_DEV
    shaped = (blocks, TOK_DEV, HEADS, HD)
    query_blocks = queries.reshape(shaped)
    key_blocks = keys.reshape(shaped)
    value_blocks = values.reshape(shaped)
    cotan_blocks = cotangent.reshape(shaped)
    rows = lax.broadcasted_iota(jnp.int32, (TOK_DEV, TOK_DEV), 0)
    cols = lax.broadcasted_iota(jnp.int32, (TOK_DEV, TOK_DEV), 1)
    causal = (cols <= rows)[None]
    highest = lax.Precision.HIGHEST

    def forward_block(carry, inputs):
        state, normal = carry
        query_rows, key_rows, value_rows, cotan_rows = inputs
        q_feat = features(query_rows).astype(jnp.bfloat16).astype(jnp.float32)
        k_feat = features(key_rows).astype(jnp.bfloat16).astype(jnp.float32)
        value_wide = value_rows.astype(jnp.float32)
        scores = jnp.einsum('thd,shd->hts', q_feat, k_feat)
        scores = jnp.where(causal, scores, 0.0)
        weights = scores.astype(jnp.bfloat16).astype(jnp.float32)
        state_low = state.astype(jnp.bfloat16).astype(jnp.float32)
        den = jnp.sum(scores, axis=2).T + jnp.einsum('thd,hd->th', q_feat, normal, precision=highest)
        num = jnp.einsum('hts,she->the', weights, value_wide) + jnp.einsum('thd,hde->the', q_feat, state_low)
        ratio = num / den[:, :, None]
        cotan_wide = cotan_rows.astype(jnp.float32)
        grad_scaled = (cotan_wide / den[:, :, None]).astype(jnp.bfloat16).astype(jnp.float32)
        grad_den = -jnp.sum(cotan_wide * ratio, axis=2) / den
        grad_scores = jnp.einsum('the,she->hts', grad_scaled, value_wide) + grad_den.T[:, :, None]
        grad_scores = jnp.where(causal, grad_scores, 0.0).astype(jnp.bfloat16).astype(jnp.float32)
        q_lin = jnp.einsum('hts,shd->thd', grad_scores, k_feat) + jnp.einsum('the,hde->thd', grad_scaled, state_low)
        q_lin = q_lin + grad_den[:, :, None] * normal[None]
        query_grad = (q_lin * slope(query_rows)).astype(jnp.bfloat16)
        new_state = state + jnp.einsum('shd,she->hde', k_feat, value_wide)
        new_normal = normal + jnp.sum(k_feat, axis=0)
        return (new_state, new_normal), (ratio.astype(jnp.bfloat16), query_grad, grad_scaled, grad_den)

    start = (jnp.zeros((HEADS, HD, HD), jnp.float32), jnp.zeros((HEADS, HD), jnp.float32))
    _, (attended, query_grad, grad_all, grad_den_all) = lax.scan(
        forward_block, start, (query_blocks, key_blocks, value_blocks, cotan_blocks))

    def backward_block(carry, inputs):
        later, later_norm = carry
        query_rows, key_rows, value_rows, grad_scaled, grad_den = inputs
        q_feat = features(query_rows).astype(jnp.bfloat16).astype(jnp.float32)
        k_feat = features(key_rows).astype(jnp.bfloat16).astype(jnp.float32)
        value_wide = value_rows.astype(jnp.float32)
        scores = jnp.where(causal, jnp.einsum('thd,shd->hts', q_feat, k_feat), 0.0)
        weights = scores.astype(jnp.bfloat16).astype(jnp.float32)
        grad_scores = jnp.einsum('the,she->hts', grad_scaled, value_wide) + grad_den.T[:, :, None]
        grad_scores = jnp.where(causal, grad_scores, 0.0).astype(jnp.bfloat16).astype(jnp.float32)
        later_low = later.astype(jnp.bfloat16).astype(jnp.float32)
        k_lin = jnp.einsum('hts,thd->shd', grad_scores, q_feat) + jnp.einsum('she,hde->shd', value_wide, later_low)
        k_lin = k_lin + later_norm[None]
        key_grad = (k_lin * slope(key_rows)).astype(jnp.bfloat16)
        value_grad = jnp.einsum('hts,the->she', weights, grad_scaled) + jnp.einsum('shd,hde->she', k_feat, later_low)
        new_later = later + jnp.einsum('thd,the->hde', q_feat, grad_scaled)
        new_norm = later_norm + jnp.einsum('th,thd->hd', grad_den, q_feat, precision=highest)
        return (new_later, new_norm), (key_grad, value_grad.astype(jnp.bfloat16))

    _, (key_grad, value_grad) = lax.scan(
        backward_block, start, (query_blocks, key_blocks, value_blocks, grad_all, grad_den_all), reverse=True)
    flat = (TOKENS, HEADS * HD)
    return (attended.reshape(flat), query_grad.reshape(flat), key_grad.reshape(flat), value_grad.reshape(flat))
```

```python
import functools

import jax
import jax.numpy as jnp
from jax import lax
from jax.experimental import pallas as pl
from jax.experimental.pallas import tpu as pltpu
from jax.sharding import PartitionSpec as P

HEADS = 16
HD = 128
MESH = pl.DeviceIdType.MESH
NZ, NX, NY = 16, 4, 4
R = 1088


def scan_kernel(rev, rz, rp, n, s_ref, p_ref, oth, uin, uout, din, dout, yin, yout, xpin, xpout, xmin, xmout, pin, pout, rs, ss):
    rows = R // n
    z = lax.axis_index("inner")
    outer = lax.axis_index("outer")
    core = lax.rem(outer, 2)
    x = lax.rem(outer // 2, NX)
    y = outer // (2 * NX)
    flip = (lambda v, m: m - 1 - v) if rev else (lambda v, m: v)
    zc, xc, yc, cc = flip(z, NZ), flip(x, NX), flip(y, NY), flip(core, 2)

    def dev(y_, x_, c_, z_):
        return {"outer": (y_ * NX + x_) * 2 + c_, "inner": z_}

    step = -1 if rev else 1
    zn = lax.rem(z + step + NZ, NZ)
    zp = lax.rem(z - step + NZ, NZ)
    xn = lax.rem(x + step + NX, NX)
    xp = lax.rem(x - step + NX, NX)
    yn = lax.rem(y + step + NY, NY)
    yp = lax.rem(y - step + NY, NY)
    d_zn, d_zp = dev(y, x, core, zn), dev(y, x, core, zp)
    d_xn, d_xp = dev(y, xn, core, z), dev(y, xp, core, z)
    d_yn, d_yp = dev(yn, x, core, z), dev(yp, x, core, z)
    d_oc = dev(y, x, 1 - core, z)

    bar = pltpu.get_barrier_semaphore()
    for d in (d_zn, d_zp, d_xn, d_xp, d_yn, d_yp, d_oc):
        pl.semaphore_signal(bar, inc=1, device_id=d, device_id_type=MESH)

    @pl.when(zc == 0)
    def _():
        uin[...] = jnp.zeros_like(uin)

    @pl.when(zc == NZ - 1)
    def _():
        din[...] = jnp.zeros_like(din)

    @pl.when(yc == 0)
    def _():
        yin[...] = jnp.zeros_like(yin)

    @pl.when(xc == 0)
    def _():
        xpin[...] = jnp.zeros_like(xpin)

    @pl.when(xc == NX - 1)
    def _():
        xmin[...] = jnp.zeros_like(xmin)

    pl.semaphore_wait(bar, 7)

    def rc(k, src, dst, d, i):
        return pltpu.make_async_remote_copy(src_ref=src, dst_ref=dst, send_sem=ss.at[k], recv_sem=rs.at[k, i], device_id=d, device_id_type=MESH)

    def cut(i):
        return pl.ds(pl.multiple_of(i * rows, 8), rows)

    def ex(i):
        return rc(0, s_ref.at[1 - core, cut(i)], oth.at[cut(i)], d_oc, i)

    def up(i):
        return rc(1, uout.at[i], uin.at[i], d_zn, i)

    def down(i):
        return rc(2, dout.at[i], din.at[i], d_zp, i)

    def yy(i):
        return rc(3, yout.at[i], yin.at[i], d_yn, i)

    def xpl(i):
        return rc(4, xpout.at[i], xpin.at[i], d_xn, i)

    def xmi(i):
        return rc(5, xmout.at[i], xmin.at[i], d_xp, i)

    def px(i):
        return rc(6, pout.at[i], pin.at[i], d_oc, i)

    @pl.loop(0, n)
    def _(i):
        ex(i).start()

    oU = rz * zc
    oD = rz * (NZ - 1 - zc)
    oY = jnp.maximum(oU, oD) + rp * yc
    oXp = oY + rp * xc
    oXm = oY + rp * (NX - 1 - xc)
    oF = jnp.maximum(oXp, oXm)
    first = jnp.minimum(oU, oD)

    def ac(i):
        own = s_ref[core, cut(i)]
        other = oth[cut(i)]
        return jnp.where(cc == 0, own, other), own + other

    def on(i, f):
        @pl.when(jnp.logical_and(i >= 0, i < n))
        def _():
            f(i)

    def sU(i):
        @pl.when(zc > 0)
        def _():
            up(i).wait_recv()

        a, c = ac(i)
        uout[i, 0] = uin[i, 0] + a
        uout[i, 1] = uin[i, 1] + c

        @pl.when(zc < NZ - 1)
        def _():
            up(i).start()

    def sD(i):
        @pl.when(zc < NZ - 1)
        def _():
            down(i).wait_recv()

        a, c = ac(i)
        dout[i, 0] = din[i, 0] + a
        dout[i, 1] = din[i, 1] + c

        @pl.when(zc > 0)
        def _():
            down(i).start()

    def sY(i):
        @pl.when(yc > 0)
        def _():
            yy(i).wait_recv()

        yout[i] = yin[i] + (uout[i, 1] + din[i, 1])

        @pl.when(yc < NY - 1)
        def _():
            yy(i).start()

    def sXp(i):
        @pl.when(xc > 0)
        def _():
            xpl(i).wait_recv()

        xpout[i] = xpin[i] + yout[i]

        @pl.when(xc < NX - 1)
        def _():
            xpl(i).start()

    def sXm(i):
        @pl.when(xc < NX - 1)
        def _():
            xmi(i).wait_recv()

        xmout[i] = xmin[i] + yin[i]

        @pl.when(xc > 0)
        def _():
            xmi(i).start()

    def sF(i):
        cc_ = xpin[i] + xmout[i]
        p0 = cc_ + uin[i, 0]
        p1 = cc_ + uin[i, 1] + dout[i, 0]
        p_ref[core, cut(i)] = jnp.where(cc == 0, p0, p1)
        pout[i] = jnp.where(cc == 0, p1, p0)
        px(i).start()

    def slot(s, carry):
        def early(i):
            ex(i).wait_recv()

        on(s - first, early)
        on(s - oU, sU)
        on(s - oD, sD)
        on(s - oY, sY)
        on(s - oXp, sXp)
        on(s - oXm, sXm)
        on(s - oF, sF)
        return carry

    lax.fori_loop(0, n + rz * (NZ - 1) + rp * (NY - 1 + NX - 1), slot, 0)

    @pl.loop(0, n)
    def _(i):
        px(i).wait_recv()
        p_ref[1 - core, cut(i)] = pin[i]

    def whole(k, buf, d):
        return pltpu.make_async_remote_copy(src_ref=buf, dst_ref=buf, send_sem=ss.at[k], recv_sem=rs.at[k, 0], device_id=d, device_id_type=MESH)

    whole(0, oth, d_oc).wait_send()

    @pl.when(zc < NZ - 1)
    def _():
        whole(1, uout, d_zn).wait_send()

    @pl.when(zc > 0)
    def _():
        whole(2, dout, d_zp).wait_send()

    @pl.when(yc < NY - 1)
    def _():
        whole(3, yout, d_yn).wait_send()

    @pl.when(xc < NX - 1)
    def _():
        whole(4, xpout, d_xn).wait_send()

    @pl.when(xc > 0)
    def _():
        whole(5, xmout, d_xp).wait_send()

    whole(6, pout, d_oc).wait_send()


def scan(s, rev, n=34, rz=4, rp=4):
    rows = R // n
    f32 = jnp.float32
    one = pltpu.VMEM((n, rows, 128), f32)
    two = pltpu.VMEM((n, 2, rows, 128), f32)
    return pl.pallas_call(
        functools.partial(scan_kernel, rev, rz, rp, n),
        out_shape=jax.ShapeDtypeStruct((2, R, 128), f32),
        in_specs=[pl.BlockSpec(memory_space=pltpu.VMEM)],
        out_specs=pl.BlockSpec(memory_space=pltpu.VMEM),
        scratch_shapes=[pltpu.VMEM((R, 128), f32), two, two, two, two, one, one, one, one, one, one, one, one,
                        pltpu.SemaphoreType.DMA((7, n)), pltpu.SemaphoreType.DMA((7,))],
        compiler_params=pltpu.CompilerParams(collective_id=1 if rev else 0, has_side_effects=True, vmem_limit_bytes=60 << 20),
        name="scan_rev" if rev else "scan_fwd",
    )(s)


def features(x):
    wide = x.astype(jnp.float32)
    return jnp.where(wide > 0, wide + 1.0, jnp.exp(jnp.minimum(wide, 0.0)))


def slope(x):
    wide = x.astype(jnp.float32)
    return jnp.where(wide > 0, 1.0, jnp.exp(jnp.minimum(wide, 0.0)))


def carry_states(parts, backward):
    state, norm = parts
    half = HEADS // 2
    norms = jnp.pad(norm.reshape(2, half, HD), ((0, 0), (0, R - half * HD - half), (0, 0)))
    both = jnp.concatenate([state.reshape(2, half * HD, HD), norms], axis=1)
    out = scan(both, backward)
    return (
        out[:, : half * HD].reshape(HEADS, HD, HD),
        out[:, half * HD : half * HD + half].reshape(HEADS, HD),
    )


def per_device(queries, keys, values, cotangent):
    count_rows = queries.shape[0]
    shaped = (count_rows, HEADS, HD)
    query_rows = queries.reshape(shaped)
    key_rows = keys.reshape(shaped)
    value_rows = values.reshape(shaped)
    cotan_rows = cotangent.reshape(shaped)
    highest = lax.Precision.HIGHEST
    f32 = jnp.float32
    rows = lax.broadcasted_iota(jnp.int32, (count_rows, count_rows), 0)
    cols = lax.broadcasted_iota(jnp.int32, (count_rows, count_rows), 1)
    causal = (cols <= rows)[None]
    q_feat = features(query_rows).astype(jnp.bfloat16)
    k_feat = features(key_rows).astype(jnp.bfloat16)
    q_wide = q_feat.astype(f32)
    scores = jnp.einsum("thd,shd->hts", q_feat, k_feat, preferred_element_type=f32)
    scores = jnp.where(causal, scores, 0.0)
    weights = scores.astype(jnp.bfloat16)
    local_state = jnp.einsum("shd,she->hde", k_feat, value_rows, preferred_element_type=f32)
    local_norm = jnp.sum(k_feat.astype(f32), axis=0)
    intra_num = jnp.einsum("hts,she->the", weights, value_rows, preferred_element_type=f32)
    intra_den = jnp.sum(scores, axis=2).T
    state, normal = carry_states((local_state, local_norm), False)
    state_low = state.astype(jnp.bfloat16)
    den = intra_den + jnp.einsum("thd,hd->th", q_wide, normal, precision=highest)
    num = intra_num + jnp.einsum("thd,hde->the", q_feat, state_low, preferred_element_type=f32)
    ratio = num / den[:, :, None]
    attended = ratio.astype(jnp.bfloat16)
    cotan_wide = cotan_rows.astype(f32)
    grad_scaled = (cotan_wide / den[:, :, None]).astype(jnp.bfloat16)
    grad_den = -jnp.sum(cotan_wide * ratio, axis=2) / den
    grad_scores = jnp.einsum("the,she->hts", grad_scaled, value_rows, preferred_element_type=f32)
    grad_scores = jnp.where(causal, grad_scores + grad_den.T[:, :, None], 0.0).astype(jnp.bfloat16)
    later_local = jnp.einsum("thd,the->hde", q_feat, grad_scaled, preferred_element_type=f32)
    later_norm_local = jnp.einsum("th,thd->hd", grad_den, q_wide, precision=highest)
    q_lin = jnp.einsum("hts,shd->thd", grad_scores, k_feat, preferred_element_type=f32)
    q_lin = q_lin + jnp.einsum("the,hde->thd", grad_scaled, state_low, preferred_element_type=f32)
    q_lin = q_lin + grad_den[:, :, None] * normal[None]
    query_grad = (q_lin * slope(query_rows)).astype(jnp.bfloat16)
    k_intra = jnp.einsum("hts,thd->shd", grad_scores, q_feat, preferred_element_type=f32)
    v_intra = jnp.einsum("hts,the->she", weights, grad_scaled, preferred_element_type=f32)
    later, later_norm = carry_states((later_local, later_norm_local), True)
    later_low = later.astype(jnp.bfloat16)
    k_lin = k_intra + jnp.einsum("she,hde->shd", value_rows, later_low, preferred_element_type=f32)
    k_lin = k_lin + later_norm[None]
    key_grad = (k_lin * slope(key_rows)).astype(jnp.bfloat16)
    value_grad = v_intra + jnp.einsum("shd,hde->she", k_feat, later_low, preferred_element_type=f32)
    flat = (count_rows, HEADS * HD)
    return (
        attended.reshape(flat),
        query_grad.reshape(flat),
        key_grad.reshape(flat),
        value_grad.astype(jnp.bfloat16).reshape(flat),
    )


def solution(mesh):
    placed = (
        P(("outer", "inner"), None),
        P(("outer", "inner"), None),
        P(("outer", "inner"), None),
        P(("outer", "inner"), None),
    )
    return jax.shard_map(
        per_device,
        mesh=mesh,
        in_specs=placed,
        out_specs=(
            P(("outer", "inner"), None),
            P(("outer", "inner"), None),
            P(("outer", "inner"), None),
            P(("outer", "inner"), None),
        ),
        check_vma=False,
    )
```

```python
import functools

import jax
import jax.numpy as jnp
from jax import lax
from jax.experimental import pallas as pl
from jax.experimental.pallas import tpu as pltpu
from jax.sharding import PartitionSpec as P

HEADS = 16
HD = 128
TOK = 128
NZ, NX, NY = 16, 4, 4
MESH = pl.DeviceIdType.MESH
CHUNK = 64
PER_HEAD = HD // CHUNK
N = 1 + HEADS * PER_HEAD
SUBSTEP = 4
F32 = jnp.float32
BF16 = jnp.bfloat16


def features(x):
    wide = x.astype(F32)
    return jnp.where(wide > 0, wide + 1.0, jnp.exp(jnp.minimum(wide, 0.0)))


def slope(x):
    wide = x.astype(F32)
    return jnp.where(wide > 0, 1.0, jnp.exp(jnp.minimum(wide, 0.0)))


def mul(a, b, da, db):
    return lax.dot_general(a, b, (((da,), (db,)), ((), ())), preferred_element_type=F32)


class Scan:
    def __init__(self, rev, s, p, bufs, rs, ss):
        self.s, self.p, self.rs, self.ss = s, p, rs, ss
        (self.oth, self.zin, self.zout, self.tin, self.yin, self.yout, self.xpin, self.xpout,
         self.xmin, self.xmout, self.cin, self.cout) = bufs
        z = lax.axis_index("inner")
        outer = lax.axis_index("outer")
        core = lax.rem(outer, 2)
        x = lax.rem(outer // 2, NX)
        y = outer // (2 * NX)
        flip = (lambda v, m: m - 1 - v) if rev else (lambda v, m: v)
        self.xc, self.yc, self.cc = flip(x, NX), flip(y, NY), flip(core, 2)
        zc = flip(z, NZ)
        step = -1 if rev else 1

        def dev(y_, x_, c_, z_):
            return {"outer": (y_ * NX + x_) * 2 + c_, "inner": z_}

        zstep = jnp.where(self.cc == 0, step, -step)
        self.zpos = jnp.where(self.cc == 0, zc, NZ - 1 - zc)
        self.d_zn = dev(y, x, core, lax.rem(z + zstep + NZ, NZ))
        self.d_zp = dev(y, x, core, lax.rem(z - zstep + NZ, NZ))
        self.d_xn = dev(y, lax.rem(x + step + NX, NX), core, z)
        self.d_xp = dev(y, lax.rem(x - step + NX, NX), core, z)
        self.d_yn = dev(lax.rem(y + step + NY, NY), x, core, z)
        self.d_yp = dev(lax.rem(y - step + NY, NY), x, core, z)
        self.d_oc = dev(y, x, 1 - core, z)

    def clear(self):
        def zero(where, ref):
            @pl.when(where)
            def _():
                ref[...] = jnp.zeros_like(ref)

        zero(self.zpos == 0, self.zin)
        zero(self.yc == 0, self.yin)
        zero(self.xc == 0, self.xpin)
        zero(self.xc == NX - 1, self.xmin)

    def rc(self, k, src, dst, d, i):
        return pltpu.make_async_remote_copy(src_ref=src, dst_ref=dst, send_sem=self.ss.at[k], recv_sem=self.rs.at[k, i], device_id=d, device_id_type=MESH)

    def ex(self, i):
        return self.rc(0, self.s.at[i], self.oth.at[i], self.d_oc, i)

    def zz(self, i):
        return self.rc(1, self.zout.at[i], self.zin.at[i], self.d_zn, i)

    def tu(self, i):
        return self.rc(2, self.zin.at[i, 1], self.tin.at[i], self.d_oc, i)

    def td(self, i):
        return self.rc(2, self.zout.at[i, 1], self.tin.at[i], self.d_oc, i)

    def yy(self, i):
        return self.rc(3, self.yout.at[i], self.yin.at[i], self.d_yn, i)

    def xpl(self, i):
        return self.rc(4, self.xpout.at[i], self.xpin.at[i], self.d_xn, i)

    def xmi(self, i):
        return self.rc(5, self.xmout.at[i], self.xmin.at[i], self.d_xp, i)

    def ce(self, i):
        return self.rc(6, self.cout.at[i], self.cin.at[i], self.d_oc, i)

    def step_z(self, i):
        cc, zin, zout = self.cc, self.zin, self.zout
        self.ex(i).wait_recv()

        @pl.when(self.zpos > 0)
        def _():
            self.zz(i).wait_recv()

        @pl.when(cc == 0)
        def _():
            self.tu(i).start()

        own = self.s[i]
        other = self.oth[i]
        zout[i, 0] = zin[i, 0] + jnp.where(cc == 0, own, other)
        zout[i, 1] = zin[i, 1] + (own + other)

        @pl.when(self.zpos < NZ - 1)
        def _():
            self.zz(i).start()

        @pl.when(jnp.logical_and(cc == 1, lax.rem(i, 2) == 0))
        def _():
            self.td(i).start()

    def step_y(self, i):
        self.tu(i).wait_recv()

        @pl.when(self.yc > 0)
        def _():
            self.yy(i).wait_recv()

        self.yout[i] = self.yin[i] + (self.tin[i] + jnp.where(self.cc == 0, self.zin[i, 1], self.zout[i, 1]))

        @pl.when(self.yc < NY - 1)
        def _():
            self.yy(i).start()

    def step_xp(self, i):
        @pl.when(self.xc > 0)
        def _():
            self.xpl(i).wait_recv()

        self.xpout[i] = self.xpin[i] + self.yout[i]

        @pl.when(self.xc < NX - 1)
        def _():
            self.xpl(i).start()

    def step_xm(self, i):
        @pl.when(self.xc < NX - 1)
        def _():
            self.xmi(i).wait_recv()

        self.xmout[i] = self.xmin[i] + self.yin[i]

        @pl.when(self.xc > 0)
        def _():
            self.xmi(i).start()

    def column(self, i):
        return jnp.where(self.cc == 0, self.zin[i, 0], self.tin[i] + self.zout[i, 0])

    def step_f(self, i):
        c = self.xpin[i] + self.xmout[i]
        self.cout[i] = c
        self.ce(i).start()
        self.p[i] = c + self.column(i)

    def run(self):
        cc = self.cc
        l_y = jnp.where(self.zpos < NZ // 2, N, 1 + SUBSTEP * self.yc)
        l_xp = l_y + SUBSTEP * self.xc
        l_xm = l_y + SUBSTEP * (NX - 1 - self.xc)
        l_f = jnp.maximum(l_xp, l_xm)

        def slot(t, carry):
            @pl.when(t < N)
            def _():
                self.step_z(t)

            def later(lag, f):
                i = t - lag

                @pl.when((i >= 0) & (i < N) & (lax.rem(i + 2 * N, 2) == cc))
                def _():
                    f(i)

            later(l_y, self.step_y)
            later(l_xp, self.step_xp)
            later(l_xm, self.step_xm)
            later(l_f, self.step_f)
            return carry

        lax.fori_loop(0, N + l_f, slot, 0)

    def finish(self, i):
        @pl.when(lax.rem(i, 2) != self.cc)
        def _():
            @pl.when(self.cc == 1)
            def _():
                self.tu(i).wait_recv()

            self.ce(i).wait_recv()
            self.p[i] = self.cin[i] + self.column(i)

    def drain(self):
        def whole(k, buf, d):
            pltpu.make_async_remote_copy(src_ref=buf, dst_ref=buf, send_sem=self.ss.at[k], recv_sem=self.rs.at[k, 0], device_id=d, device_id_type=MESH).wait_send()

        def mine(k, buf, d, where):
            @pl.when(where & (self.cc == 0))
            def _():
                whole(k, buf.at[pl.ds(0, N - N // 2)], d)

            @pl.when(where & (self.cc == 1))
            def _():
                whole(k, buf.at[pl.ds(0, N // 2)], d)

        whole(0, self.oth, self.d_oc)

        @pl.when(self.zpos < NZ - 1)
        def _():
            whole(1, self.zout, self.d_zn)

        @pl.when(self.cc == 0)
        def _():
            whole(2, self.tin, self.d_oc)

        @pl.when(self.cc == 1)
        def _():
            whole(2, self.tin.at[pl.ds(0, N - N // 2)], self.d_oc)

        mine(3, self.yout, self.d_yn, self.yc < NY - 1)
        mine(4, self.xpout, self.d_xn, self.xc < NX - 1)
        mine(5, self.xmout, self.d_xp, self.xc > 0)
        mine(6, self.cout, self.d_oc, self.cc >= 0)


N_BUFS = 12


def kernel(q_ref, k_ref, v_ref, g_ref, att_ref, qg_ref, kg_ref, vg_ref, qf_ref, kf_ref, ki_ref, vi_ref, s1, p1, s2, p2, *rest):
    bufs1, bufs2 = rest[:N_BUFS], rest[N_BUFS : 2 * N_BUFS]
    rs1, ss1, rs2, ss2 = rest[2 * N_BUFS :]
    one = Scan(False, s1, p1, bufs1, rs1, ss1)
    two = Scan(True, s2, p2, bufs2, rs2, ss2)
    near = (one.d_zn, one.d_zp, one.d_xn, one.d_xp, one.d_yn, one.d_yp, one.d_oc)
    bar = pltpu.get_barrier_semaphore()
    for d in near:
        pl.semaphore_signal(bar, inc=1, device_id=d, device_id_type=MESH)
    s1[0] = jnp.zeros((CHUNK, HD), F32)
    s2[0] = jnp.zeros((CHUNK, HD), F32)

    def cols(h):
        return pl.ds(pl.multiple_of(h * HD, HD), HD)

    def put(s, h, state):
        for j in range(PER_HEAD):
            s[1 + h * PER_HEAD + j] = state[j * CHUNK : (j + 1) * CHUNK]

    def get(p, h):
        return jnp.concatenate([p[1 + h * PER_HEAD + j] for j in range(PER_HEAD)], axis=0)

    @pl.loop(0, HEADS)
    def _(h):
        kf = features(k_ref[:, cols(h)]).astype(BF16)
        kf_ref[:, cols(h)] = kf
        qf_ref[:, cols(h)] = features(q_ref[:, cols(h)]).astype(BF16)
        s1[0, pl.ds(h, 1), :] = jnp.sum(kf.astype(F32), axis=0, keepdims=True)
        put(s1, h, mul(kf, v_ref[:, cols(h)], 0, 0))

    one.clear()
    two.clear()
    pl.semaphore_wait(bar, len(near))

    @pl.loop(0, N)
    def _(i):
        one.ex(i).start()

    one.run()
    one.finish(0)
    rows = lax.broadcasted_iota(jnp.int32, (TOK, TOK), 0)
    lanes = lax.broadcasted_iota(jnp.int32, (TOK, TOK), 1)
    causal = lanes <= rows

    @pl.loop(0, HEADS)
    def _(h):
        for j in range(PER_HEAD):
            one.finish(1 + h * PER_HEAD + j)
        c = cols(h)
        qf, kf, v = qf_ref[:, c], kf_ref[:, c], v_ref[:, c]
        wide_q = qf.astype(F32)
        normal = p1[0, pl.ds(h, 1), :]
        low = get(p1, h).astype(BF16)
        scores = jnp.where(causal, mul(qf, kf, 1, 1), 0.0)
        weights = scores.astype(BF16)
        den = jnp.sum(scores, axis=1, keepdims=True) + jnp.sum(wide_q * normal, axis=1, keepdims=True)
        num = mul(weights, v, 1, 0) + mul(qf, low, 1, 0)
        ratio = num / den
        att_ref[:, c] = ratio.astype(BF16)
        cot = g_ref[:, c].astype(F32)
        scaled = (cot / den).astype(BF16)
        grad_den = -jnp.sum(cot * ratio, axis=1, keepdims=True) / den
        grad_scores = jnp.where(causal, mul(scaled, v, 1, 1) + grad_den, 0.0).astype(BF16)
        put(s2, h, mul(qf, scaled, 0, 0))
        s2[0, pl.ds(h, 1), :] = jnp.sum(grad_den * wide_q, axis=0, keepdims=True)
        for j in range(PER_HEAD):
            two.ex(1 + h * PER_HEAD + j).start()
        lin = mul(grad_scores, kf, 1, 0) + mul(scaled, low, 1, 1) + grad_den * normal
        qg_ref[:, c] = (lin * slope(q_ref[:, c])).astype(BF16)
        ki_ref[:, c] = mul(grad_scores, qf, 0, 0)
        vi_ref[:, c] = mul(weights, scaled, 0, 0)

    two.ex(0).start()
    two.run()
    two.finish(0)

    @pl.loop(0, HEADS)
    def _(h):
        for j in range(PER_HEAD):
            two.finish(1 + h * PER_HEAD + j)
        c = cols(h)
        low = get(p2, h).astype(BF16)
        lin = ki_ref[:, c] + mul(v_ref[:, c], low, 1, 1) + p2[0, pl.ds(h, 1), :]
        kg_ref[:, c] = (lin * slope(k_ref[:, c])).astype(BF16)
        vg_ref[:, c] = (vi_ref[:, c] + mul(kf_ref[:, c], low, 1, 0)).astype(BF16)

    one.drain()
    two.drain()


def per_device(queries, keys, values, cotangent):
    wide = HEADS * HD
    single = pltpu.VMEM((N, CHUNK, HD), F32)
    double = pltpu.VMEM((N, 2, CHUNK, HD), F32)
    bufs = [single, double, double] + [single] * (N_BUFS - 3)
    low = pltpu.VMEM((TOK, wide), BF16)
    full = pltpu.VMEM((TOK, wide), F32)
    sems = [pltpu.SemaphoreType.DMA((7, N)), pltpu.SemaphoreType.DMA((7,))]
    vmem = pl.BlockSpec(memory_space=pltpu.VMEM)
    return pl.pallas_call(
        kernel,
        out_shape=[jax.ShapeDtypeStruct((TOK, wide), BF16)] * 4,
        in_specs=[vmem] * 4,
        out_specs=[vmem] * 4,
        scratch_shapes=[low, low, full, full] + [single] * 4 + bufs * 2 + sems * 2,
        compiler_params=pltpu.CompilerParams(collective_id=0, has_side_effects=True, vmem_limit_bytes=63 << 20),
        name="linear_attention",
    )(queries, keys, values, cotangent)


def solution(mesh):
    spec = P(("outer", "inner"), None)
    return jax.shard_map(per_device, mesh=mesh, in_specs=(spec,) * 4, out_specs=(spec,) * 4, check_vma=False)
```

```python
import functools

import jax
import jax.numpy as jnp
from jax import lax
from jax.experimental import pallas as pl
from jax.experimental.pallas import tpu as pltpu
from jax.sharding import PartitionSpec as P

HEADS = 16
HD = 128
TOK = 128
NZ, NX, NY = 16, 4, 4
MESH = pl.DeviceIdType.MESH
CHUNK = 64
PER_HEAD = HD // CHUNK
N = 1 + HEADS * PER_HEAD
SUBSTEP = 3
EARLY = 50
F32 = jnp.float32
BF16 = jnp.bfloat16


def features(x):
    wide = x.astype(F32)
    return jnp.where(wide > 0, wide + 1.0, jnp.exp(jnp.minimum(wide, 0.0)))


def slope(x):
    wide = x.astype(F32)
    return jnp.where(wide > 0, 1.0, jnp.exp(jnp.minimum(wide, 0.0)))


def mul(a, b, da, db):
    return lax.dot_general(a, b, (((da,), (db,)), ((), ())), preferred_element_type=F32)


class Scan:
    def __init__(self, rev, s, p, bufs, rs, ss):
        self.s, self.p, self.rs, self.ss = s, p, rs, ss
        (self.oth, self.zin, self.zout, self.tin, self.yin, self.yout, self.xpin, self.xpout,
         self.xmin, self.xmout, self.cin, self.cout) = bufs
        z = lax.axis_index("inner")
        outer = lax.axis_index("outer")
        core = lax.rem(outer, 2)
        x = lax.rem(outer // 2, NX)
        y = outer // (2 * NX)
        flip = (lambda v, m: m - 1 - v) if rev else (lambda v, m: v)
        self.xc, self.yc, self.cc = flip(x, NX), flip(y, NY), flip(core, 2)
        zc = flip(z, NZ)
        step = -1 if rev else 1

        def dev(y_, x_, c_, z_):
            return {"outer": (y_ * NX + x_) * 2 + c_, "inner": z_}

        zstep = jnp.where(self.cc == 0, step, -step)
        self.zpos = jnp.where(self.cc == 0, zc, NZ - 1 - zc)
        self.d_zn = dev(y, x, core, lax.rem(z + zstep + NZ, NZ))
        self.d_zp = dev(y, x, core, lax.rem(z - zstep + NZ, NZ))
        self.d_xn = dev(y, lax.rem(x + step + NX, NX), core, z)
        self.d_xp = dev(y, lax.rem(x - step + NX, NX), core, z)
        self.d_yn = dev(lax.rem(y + step + NY, NY), x, core, z)
        self.d_yp = dev(lax.rem(y - step + NY, NY), x, core, z)
        self.d_oc = dev(y, x, 1 - core, z)

    def clear(self):
        def zero(where, ref):
            @pl.when(where)
            def _():
                ref[...] = jnp.zeros_like(ref)

        zero(self.zpos == 0, self.zin)
        zero(self.yc == 0, self.yin)
        zero(self.xc == 0, self.xpin)
        zero(self.xc == NX - 1, self.xmin)

    def rc(self, k, src, dst, d, i):
        return pltpu.make_async_remote_copy(src_ref=src, dst_ref=dst, send_sem=self.ss.at[k], recv_sem=self.rs.at[k, i], device_id=d, device_id_type=MESH)

    def ex(self, i):
        return self.rc(0, self.s.at[i], self.oth.at[i], self.d_oc, i)

    def zz(self, i):
        return self.rc(1, self.zout.at[i], self.zin.at[i], self.d_zn, i)

    def tu(self, i):
        return self.rc(2, self.zin.at[i, 1], self.tin.at[i], self.d_oc, i)

    def td(self, i):
        return self.rc(2, self.zout.at[i, 1], self.tin.at[i], self.d_oc, i)

    def yy(self, i):
        return self.rc(3, self.yout.at[i], self.yin.at[i], self.d_yn, i)

    def xpl(self, i):
        return self.rc(4, self.xpout.at[i], self.xpin.at[i], self.d_xn, i)

    def xmi(self, i):
        return self.rc(5, self.xmout.at[i], self.xmin.at[i], self.d_xp, i)

    def ce(self, i):
        return self.rc(6, self.cout.at[i], self.cin.at[i], self.d_oc, i)

    def step_z(self, i):
        cc, zin, zout = self.cc, self.zin, self.zout
        self.ex(i).wait_recv()

        @pl.when(self.zpos > 0)
        def _():
            self.zz(i).wait_recv()

        @pl.when(cc == 0)
        def _():
            self.tu(i).start()

        own = self.s[i]
        other = self.oth[i]
        zout[i, 0] = zin[i, 0] + jnp.where(cc == 0, own, other)
        zout[i, 1] = zin[i, 1] + (own + other)

        @pl.when(self.zpos < NZ - 1)
        def _():
            self.zz(i).start()

        @pl.when(jnp.logical_and(cc == 1, lax.rem(i, 2) == 0))
        def _():
            self.td(i).start()

    def step_y(self, i):
        self.tu(i).wait_recv()

        @pl.when(self.yc > 0)
        def _():
            self.yy(i).wait_recv()

        self.yout[i] = self.yin[i] + (self.tin[i] + jnp.where(self.cc == 0, self.zin[i, 1], self.zout[i, 1]))

        @pl.when(self.yc < NY - 1)
        def _():
            self.yy(i).start()

    def step_xp(self, i):
        @pl.when(self.xc > 0)
        def _():
            self.xpl(i).wait_recv()

        self.xpout[i] = self.xpin[i] + self.yout[i]

        @pl.when(self.xc < NX - 1)
        def _():
            self.xpl(i).start()

    def step_xm(self, i):
        @pl.when(self.xc < NX - 1)
        def _():
            self.xmi(i).wait_recv()

        self.xmout[i] = self.xmin[i] + self.yin[i]

        @pl.when(self.xc > 0)
        def _():
            self.xmi(i).start()

    def column(self, i):
        return jnp.where(self.cc == 0, self.zin[i, 0], self.tin[i] + self.zout[i, 0])

    def step_f(self, i):
        c = self.xpin[i] + self.xmout[i]
        self.cout[i] = c
        self.ce(i).start()
        self.p[i] = c + self.column(i)

    def lags(self):
        late = self.zpos >= NZ // 2
        l_y = jnp.where(late, 1, jnp.minimum(N, EARLY * (NZ - 1 - 2 * self.zpos))) + SUBSTEP * self.yc
        l_xp = l_y + SUBSTEP * self.xc
        l_xm = l_y + SUBSTEP * (NX - 1 - self.xc)
        return l_y, l_xp, l_xm, jnp.maximum(l_xp, l_xm)

    def slot(self, t):
        @pl.when((t >= 0) & (t < N))
        def _():
            self.step_z(t)

        def later(lag, f):
            i = t - lag

            @pl.when((i >= 0) & (i < N) & (lax.rem(i + 8 * N, 2) == self.cc))
            def _():
                f(i)

        l_y, l_xp, l_xm, l_f = self.lags()
        later(l_y, self.step_y)
        later(l_xp, self.step_xp)
        later(l_xm, self.step_xm)
        later(l_f, self.step_f)

    def finish(self, i):
        @pl.when(lax.rem(i, 2) != self.cc)
        def _():
            @pl.when(self.cc == 1)
            def _():
                self.tu(i).wait_recv()

            self.ce(i).wait_recv()
            self.p[i] = self.cin[i] + self.column(i)

    def drain(self):
        def whole(k, buf, d):
            pltpu.make_async_remote_copy(src_ref=buf, dst_ref=buf, send_sem=self.ss.at[k], recv_sem=self.rs.at[k, 0], device_id=d, device_id_type=MESH).wait_send()

        def mine(k, buf, d, where):
            @pl.when(where & (self.cc == 0))
            def _():
                whole(k, buf.at[pl.ds(0, N - N // 2)], d)

            @pl.when(where & (self.cc == 1))
            def _():
                whole(k, buf.at[pl.ds(0, N // 2)], d)

        whole(0, self.oth, self.d_oc)

        @pl.when(self.zpos < NZ - 1)
        def _():
            whole(1, self.zout, self.d_zn)

        @pl.when(self.cc == 0)
        def _():
            whole(2, self.tin, self.d_oc)

        @pl.when(self.cc == 1)
        def _():
            whole(2, self.tin.at[pl.ds(0, N - N // 2)], self.d_oc)

        mine(3, self.yout, self.d_yn, self.yc < NY - 1)
        mine(4, self.xpout, self.d_xn, self.xc < NX - 1)
        mine(5, self.xmout, self.d_xp, self.xc > 0)
        mine(6, self.cout, self.d_oc, self.cc >= 0)


N_BUFS = 12


def kernel(q_ref, k_ref, v_ref, g_ref, att_ref, qg_ref, kg_ref, vg_ref, qf_ref, kf_ref, ki_ref, vi_ref, s1, p1, s2, p2, *rest):
    bufs1, bufs2 = rest[:N_BUFS], rest[N_BUFS : 2 * N_BUFS]
    rs1, ss1, rs2, ss2 = rest[2 * N_BUFS :]
    one = Scan(False, s1, p1, bufs1, rs1, ss1)
    two = Scan(True, s2, p2, bufs2, rs2, ss2)
    near = (one.d_zn, one.d_zp, one.d_xn, one.d_xp, one.d_yn, one.d_yp, one.d_oc)
    bar = pltpu.get_barrier_semaphore()
    for d in near:
        pl.semaphore_signal(bar, inc=1, device_id=d, device_id_type=MESH)
    s1[0] = jnp.zeros((CHUNK, HD), F32)
    s2[N - 1] = jnp.zeros((CHUNK, HD), F32)

    def cols(h):
        return pl.ds(pl.multiple_of(h * HD, HD), HD)

    def put(s, i, state):
        for j in range(PER_HEAD):
            s[i + j] = state[j * CHUNK : (j + 1) * CHUNK]

    def get(p, i):
        return jnp.concatenate([p[i + j] for j in range(PER_HEAD)], axis=0)

    @pl.loop(0, HEADS)
    def _(h):
        kf = features(k_ref[:, cols(h)]).astype(BF16)
        kf_ref[:, cols(h)] = kf
        qf_ref[:, cols(h)] = features(q_ref[:, cols(h)]).astype(BF16)
        s1[0, pl.ds(h, 1), :] = jnp.sum(kf.astype(F32), axis=0, keepdims=True)
        put(s1, 1 + h * PER_HEAD, mul(kf, v_ref[:, cols(h)], 0, 0))

    one.clear()
    two.clear()
    pl.semaphore_wait(bar, len(near))

    @pl.loop(0, N)
    def _(i):
        one.ex(i).start()

    rows = lax.broadcasted_iota(jnp.int32, (TOK, TOK), 0)
    lanes = lax.broadcasted_iota(jnp.int32, (TOK, TOK), 1)
    causal = lanes <= rows

    def middle(h):
        c = cols(h)
        qf, kf, v = qf_ref[:, c], kf_ref[:, c], v_ref[:, c]
        wide_q = qf.astype(F32)
        normal = p1[0, pl.ds(h, 1), :]
        low = get(p1, 1 + h * PER_HEAD).astype(BF16)
        scores = jnp.where(causal, mul(qf, kf, 1, 1), 0.0)
        weights = scores.astype(BF16)
        den = jnp.sum(scores, axis=1, keepdims=True) + jnp.sum(wide_q * normal, axis=1, keepdims=True)
        num = mul(weights, v, 1, 0) + mul(qf, low, 1, 0)
        ratio = num / den
        att_ref[:, c] = ratio.astype(BF16)
        cot = g_ref[:, c].astype(F32)
        scaled = (cot / den).astype(BF16)
        grad_den = -jnp.sum(cot * ratio, axis=1, keepdims=True) / den
        put(s2, h * PER_HEAD, mul(qf, scaled, 0, 0))
        s2[N - 1, pl.ds(h, 1), :] = jnp.sum(grad_den * wide_q, axis=0, keepdims=True)
        for j in range(PER_HEAD):
            two.ex(h * PER_HEAD + j).start()

        @pl.when(h == HEADS - 1)
        def _():
            two.ex(N - 1).start()

        grad_scores = jnp.where(causal, mul(scaled, v, 1, 1) + grad_den, 0.0).astype(BF16)
        lin = mul(grad_scores, kf, 1, 0) + mul(scaled, low, 1, 1) + grad_den * normal
        qg_ref[:, c] = (lin * slope(q_ref[:, c])).astype(BF16)
        ki_ref[:, c] = mul(grad_scores, qf, 0, 0)
        vi_ref[:, c] = mul(weights, scaled, 0, 0)

    def last(h):
        c = cols(h)
        low = get(p2, h * PER_HEAD).astype(BF16)
        ki_ref[:, c] += mul(v_ref[:, c], low, 1, 1)
        vg_ref[:, c] = (vi_ref[:, c] + mul(kf_ref[:, c], low, 1, 0)).astype(BF16)

    zpos = one.zpos
    late = zpos >= NZ // 2
    behind = 2 * zpos - (NZ - 1)
    l_f1, l_f2 = one.lags()[3], two.lags()[3]
    l_g1 = l_f1 + 1 + jnp.where(late, jnp.maximum(0, N - 4 * behind // 2), 0)
    l_b = l_g1 + 6 + jnp.where(late, jnp.minimum(N, 18 + 5 * (zpos - NZ // 2)), jnp.minimum(6 * zpos, 14))
    l_g2 = l_b + l_f2 + 2 + jnp.where(late, jnp.maximum(0, N - 6 * behind // 2), 0)

    def slot(t, carry):
        one.slot(t)
        i = t - l_g1

        @pl.when((i >= 0) & (i < N))
        def _():
            one.finish(i)

            @pl.when((i > 0) & (lax.rem(i, PER_HEAD) == 0))
            def _():
                middle(i // PER_HEAD - 1)

        two.slot(t - l_b)
        k = t - l_g2

        @pl.when((k >= 0) & (k < N))
        def _():
            two.finish(k)

            @pl.when((k < N - 1) & (lax.rem(k + 1, PER_HEAD) == 0))
            def _():
                last(k // PER_HEAD)

        return carry

    lax.fori_loop(0, N + l_g2, slot, 0)

    @pl.loop(0, HEADS)
    def _(h):
        c = cols(h)
        kg_ref[:, c] = ((ki_ref[:, c] + p2[N - 1, pl.ds(h, 1), :]) * slope(k_ref[:, c])).astype(BF16)

    one.drain()
    two.drain()


def per_device(queries, keys, values, cotangent):
    wide = HEADS * HD
    single = pltpu.VMEM((N, CHUNK, HD), F32)
    double = pltpu.VMEM((N, 2, CHUNK, HD), F32)
    bufs = [single, double, double] + [single] * (N_BUFS - 3)
    low = pltpu.VMEM((TOK, wide), BF16)
    full = pltpu.VMEM((TOK, wide), F32)
    sems = [pltpu.SemaphoreType.DMA((7, N)), pltpu.SemaphoreType.DMA((7,))]
    vmem = pl.BlockSpec(memory_space=pltpu.VMEM)
    return pl.pallas_call(
        kernel,
        out_shape=[jax.ShapeDtypeStruct((TOK, wide), BF16)] * 4,
        in_specs=[vmem] * 4,
        out_specs=[vmem] * 4,
        scratch_shapes=[low, low, full, full] + [single] * 4 + bufs * 2 + sems * 2,
        compiler_params=pltpu.CompilerParams(collective_id=0, has_side_effects=True, vmem_limit_bytes=63 << 20),
        name="linear_attention",
    )(queries, keys, values, cotangent)


def solution(mesh):
    spec = P(("outer", "inner"), None)
    return jax.shard_map(per_device, mesh=mesh, in_specs=(spec,) * 4, out_specs=(spec,) * 4, check_vma=False)
```

```python
import functools

import jax
import jax.numpy as jnp
from jax import lax
from jax.experimental import pallas as pl
from jax.experimental.pallas import tpu as pltpu
from jax.sharding import PartitionSpec as P

HEADS = 16
HD = 128
TOK = 128
NZ, NX, NY = 16, 4, 4
MESH = pl.DeviceIdType.MESH
CHUNK = 64
PER_HEAD = HD // CHUNK
N = 1 + HEADS * PER_HEAD
SUBSTEP = 3
EARLY = 50
F32 = jnp.float32
BF16 = jnp.bfloat16


def features(x):
    wide = x.astype(F32)
    return jnp.where(wide > 0, wide + 1.0, jnp.exp(jnp.minimum(wide, 0.0)))


def slope(x):
    wide = x.astype(F32)
    return jnp.where(wide > 0, 1.0, jnp.exp(jnp.minimum(wide, 0.0)))


def mul(a, b, da, db):
    return lax.dot_general(a, b, (((da,), (db,)), ((), ())), preferred_element_type=F32)


class Scan:
    def __init__(self, rev, s, p, bufs, rs, ss):
        self.s, self.p, self.rs, self.ss = s, p, rs, ss
        (self.oth, self.zin, self.zout, self.tin, self.yin, self.yout, self.xpin, self.xpout,
         self.xmin, self.xmout, self.cin, self.cout) = bufs
        z = lax.axis_index("inner")
        outer = lax.axis_index("outer")
        core = lax.rem(outer, 2)
        x = lax.rem(outer // 2, NX)
        y = outer // (2 * NX)
        flip = (lambda v, m: m - 1 - v) if rev else (lambda v, m: v)
        self.xc, self.yc, self.cc = flip(x, NX), flip(y, NY), flip(core, 2)
        zc = flip(z, NZ)
        step = -1 if rev else 1

        def dev(y_, x_, c_, z_):
            return {"outer": (y_ * NX + x_) * 2 + c_, "inner": z_}

        zstep = jnp.where(self.cc == 0, step, -step)
        self.zpos = jnp.where(self.cc == 0, zc, NZ - 1 - zc)
        self.d_zn = dev(y, x, core, lax.rem(z + zstep + NZ, NZ))
        self.d_zp = dev(y, x, core, lax.rem(z - zstep + NZ, NZ))
        self.d_xn = dev(y, lax.rem(x + step + NX, NX), core, z)
        self.d_xp = dev(y, lax.rem(x - step + NX, NX), core, z)
        self.d_yn = dev(lax.rem(y + step + NY, NY), x, core, z)
        self.d_yp = dev(lax.rem(y - step + NY, NY), x, core, z)
        self.d_oc = dev(y, x, 1 - core, z)

    def clear(self):
        def zero(where, ref):
            @pl.when(where)
            def _():
                ref[...] = jnp.zeros_like(ref)

        zero(self.zpos == 0, self.zin)
        zero(self.yc == 0, self.yin)
        zero(self.xc == 0, self.xpin)
        zero(self.xc == NX - 1, self.xmin)

    def rc(self, k, src, dst, d, i):
        return pltpu.make_async_remote_copy(src_ref=src, dst_ref=dst, send_sem=self.ss.at[k], recv_sem=self.rs.at[k, i], device_id=d, device_id_type=MESH)

    def ex(self, i):
        return self.rc(0, self.s.at[i], self.oth.at[i], self.d_oc, i)

    def zz(self, i):
        return self.rc(1, self.zout.at[i], self.zin.at[i], self.d_zn, i)

    def tu(self, i):
        return self.rc(2, self.zin.at[i, 1], self.tin.at[i], self.d_oc, i)

    def td(self, i):
        return self.rc(2, self.zout.at[i, 1], self.tin.at[i], self.d_oc, i)

    def yy(self, i):
        return self.rc(3, self.yout.at[i], self.yin.at[i], self.d_yn, i)

    def xpl(self, i):
        return self.rc(4, self.xpout.at[i], self.xpin.at[i], self.d_xn, i)

    def xmi(self, i):
        return self.rc(5, self.xmout.at[i], self.xmin.at[i], self.d_xp, i)

    def ce(self, i):
        return self.rc(6, self.cout.at[i], self.cin.at[i], self.d_oc, i)

    def step_z(self, i):
        cc, zin, zout = self.cc, self.zin, self.zout
        self.ex(i).wait_recv()

        @pl.when(self.zpos > 0)
        def _():
            self.zz(i).wait_recv()

        @pl.when(cc == 0)
        def _():
            self.tu(i).start()

        own = self.s[i]
        other = self.oth[i]
        zout[i, 0] = zin[i, 0] + jnp.where(cc == 0, own, other)
        zout[i, 1] = zin[i, 1] + (own + other)

        @pl.when(self.zpos < NZ - 1)
        def _():
            self.zz(i).start()

        @pl.when(jnp.logical_and(cc == 1, lax.rem(i, 2) == 0))
        def _():
            self.td(i).start()

    def step_y(self, i):
        self.tu(i).wait_recv()

        @pl.when(self.yc > 0)
        def _():
            self.yy(i).wait_recv()

        self.yout[i] = self.yin[i] + (self.tin[i] + jnp.where(self.cc == 0, self.zin[i, 1], self.zout[i, 1]))

        @pl.when(self.yc < NY - 1)
        def _():
            self.yy(i).start()

    def step_xp(self, i):
        @pl.when(self.xc > 0)
        def _():
            self.xpl(i).wait_recv()

        self.xpout[i] = self.xpin[i] + self.yout[i]

        @pl.when(self.xc < NX - 1)
        def _():
            self.xpl(i).start()

    def step_xm(self, i):
        @pl.when(self.xc < NX - 1)
        def _():
            self.xmi(i).wait_recv()

        self.xmout[i] = self.xmin[i] + self.yin[i]

        @pl.when(self.xc > 0)
        def _():
            self.xmi(i).start()

    def column(self, i):
        return jnp.where(self.cc == 0, self.zin[i, 0], self.tin[i] + self.zout[i, 0])

    def step_f(self, i):
        c = self.xpin[i] + self.xmout[i]
        self.cout[i] = c
        self.ce(i).start()
        self.p[i] = c + self.column(i)

    def lags(self):
        late = self.zpos >= NZ // 2
        l_y = jnp.where(late, 1, jnp.minimum(N, EARLY * (NZ - 1 - 2 * self.zpos))) + SUBSTEP * self.yc
        l_xp = l_y + SUBSTEP * self.xc
        l_xm = l_y + SUBSTEP * (NX - 1 - self.xc)
        return l_y, l_xp, l_xm, jnp.maximum(l_xp, l_xm)

    def slot(self, t):
        @pl.when((t >= 0) & (t < N))
        def _():
            self.step_z(t)

        def later(lag, f):
            i = t - lag

            @pl.when((i >= 0) & (i < N) & (lax.rem(i + 8 * N, 2) == self.cc))
            def _():
                f(i)

        l_y, l_xp, l_xm, l_f = self.lags()
        later(l_y, self.step_y)
        later(l_xp, self.step_xp)
        later(l_xm, self.step_xm)
        later(l_f, self.step_f)

    def finish(self, i):
        @pl.when(lax.rem(i, 2) != self.cc)
        def _():
            @pl.when(self.cc == 1)
            def _():
                self.tu(i).wait_recv()

            self.ce(i).wait_recv()
            self.p[i] = self.cin[i] + self.column(i)

    def drain(self):
        def whole(k, buf, d):
            pltpu.make_async_remote_copy(src_ref=buf, dst_ref=buf, send_sem=self.ss.at[k], recv_sem=self.rs.at[k, 0], device_id=d, device_id_type=MESH).wait_send()

        def mine(k, buf, d, where):
            @pl.when(where & (self.cc == 0))
            def _():
                whole(k, buf.at[pl.ds(0, N - N // 2)], d)

            @pl.when(where & (self.cc == 1))
            def _():
                whole(k, buf.at[pl.ds(0, N // 2)], d)

        whole(0, self.oth, self.d_oc)

        @pl.when(self.zpos < NZ - 1)
        def _():
            whole(1, self.zout, self.d_zn)

        @pl.when(self.cc == 0)
        def _():
            whole(2, self.tin, self.d_oc)

        @pl.when(self.cc == 1)
        def _():
            whole(2, self.tin.at[pl.ds(0, N - N // 2)], self.d_oc)

        mine(3, self.yout, self.d_yn, self.yc < NY - 1)
        mine(4, self.xpout, self.d_xn, self.xc < NX - 1)
        mine(5, self.xmout, self.d_xp, self.xc > 0)
        mine(6, self.cout, self.d_oc, self.cc >= 0)


N_BUFS = 12


def kernel(q_ref, k_ref, v_ref, g_ref, att_ref, qg_ref, kg_ref, vg_ref, qf_ref, kf_ref, ki_ref, vi_ref, w_ref, gs_ref, den_ref, gd_ref, s1, p1, s2, p2, *rest):
    bufs1, bufs2 = rest[:N_BUFS], rest[N_BUFS : 2 * N_BUFS]
    rs1, ss1, rs2, ss2 = rest[2 * N_BUFS :]
    one = Scan(False, s1, p1, bufs1, rs1, ss1)
    two = Scan(True, s2, p2, bufs2, rs2, ss2)
    near = (one.d_zn, one.d_zp, one.d_xn, one.d_xp, one.d_yn, one.d_yp, one.d_oc)
    bar = pltpu.get_barrier_semaphore()
    for d in near:
        pl.semaphore_signal(bar, inc=1, device_id=d, device_id_type=MESH)
    s1[0] = jnp.zeros((CHUNK, HD), F32)
    s2[N - 1] = jnp.zeros((CHUNK, HD), F32)

    def cols(h):
        return pl.ds(pl.multiple_of(h * HD, HD), HD)

    def put(s, i, state):
        for j in range(PER_HEAD):
            s[i + j] = state[j * CHUNK : (j + 1) * CHUNK]

    def get(p, i):
        return jnp.concatenate([p[i + j] for j in range(PER_HEAD)], axis=0)

    @pl.loop(0, HEADS)
    def _(h):
        kf = features(k_ref[:, cols(h)]).astype(BF16)
        kf_ref[:, cols(h)] = kf
        qf_ref[:, cols(h)] = features(q_ref[:, cols(h)]).astype(BF16)
        s1[0, pl.ds(h, 1), :] = jnp.sum(kf.astype(F32), axis=0, keepdims=True)
        put(s1, 1 + h * PER_HEAD, mul(kf, v_ref[:, cols(h)], 0, 0))

    one.clear()
    two.clear()
    pl.semaphore_wait(bar, len(near))

    @pl.loop(0, N)
    def _(i):
        one.ex(i).start()

    rows = lax.broadcasted_iota(jnp.int32, (TOK, TOK), 0)
    lanes = lax.broadcasted_iota(jnp.int32, (TOK, TOK), 1)
    causal = lanes <= rows

    def before(h):
        c = cols(h)
        scores = jnp.where(causal, mul(qf_ref[:, c], kf_ref[:, c], 1, 1), 0.0)
        weights = scores.astype(BF16)
        w_ref[:, c] = weights
        den_ref[h] = jnp.sum(scores, axis=1, keepdims=True)
        vi_ref[:, c] = mul(weights, v_ref[:, c], 1, 0)

    def middle(h):
        c = cols(h)
        qf = qf_ref[:, c]
        wide_q = qf.astype(F32)
        normal = p1[0, pl.ds(h, 1), :]
        low = get(p1, 1 + h * PER_HEAD).astype(BF16)
        den = den_ref[h] + jnp.sum(wide_q * normal, axis=1, keepdims=True)
        num = vi_ref[:, c] + mul(qf, low, 1, 0)
        ratio = num / den
        att_ref[:, c] = ratio.astype(BF16)
        cot = g_ref[:, c].astype(F32)
        scaled = (cot / den).astype(BF16)
        grad_den = -jnp.sum(cot * ratio, axis=1, keepdims=True) / den
        gs_ref[:, c] = scaled
        gd_ref[h] = grad_den
        put(s2, h * PER_HEAD, mul(qf, scaled, 0, 0))
        s2[N - 1, pl.ds(h, 1), :] = jnp.sum(grad_den * wide_q, axis=0, keepdims=True)
        for j in range(PER_HEAD):
            two.ex(h * PER_HEAD + j).start()

        @pl.when(h == HEADS - 1)
        def _():
            two.ex(N - 1).start()

    def after(h):
        c = cols(h)
        qf, kf, v, scaled, grad_den = qf_ref[:, c], kf_ref[:, c], v_ref[:, c], gs_ref[:, c], gd_ref[h]
        normal = p1[0, pl.ds(h, 1), :]
        low = get(p1, 1 + h * PER_HEAD).astype(BF16)
        grad_scores = jnp.where(causal, mul(scaled, v, 1, 1) + grad_den, 0.0).astype(BF16)
        lin = mul(grad_scores, kf, 1, 0) + mul(scaled, low, 1, 1) + grad_den * normal
        qg_ref[:, c] = (lin * slope(q_ref[:, c])).astype(BF16)
        ki_ref[:, c] = mul(grad_scores, qf, 0, 0)
        vi_ref[:, c] = mul(w_ref[:, c], scaled, 0, 0)

    def last(h):
        c = cols(h)
        low = get(p2, h * PER_HEAD).astype(BF16)
        ki_ref[:, c] += mul(v_ref[:, c], low, 1, 1)
        vg_ref[:, c] = (vi_ref[:, c] + mul(kf_ref[:, c], low, 1, 0)).astype(BF16)

    zpos = one.zpos
    late = zpos >= NZ // 2
    behind = 2 * zpos - (NZ - 1)
    l_f1, l_f2 = one.lags()[3], two.lags()[3]
    l_g1 = l_f1 + 1 + jnp.where(late, jnp.maximum(0, N - 4 * behind // 2), 0)
    l_b = l_g1 + 6 + jnp.where(late, jnp.minimum(N, 33 + 5 * (zpos - NZ // 2)), jnp.minimum(6 * zpos, 33))
    l_g2 = l_b + l_f2 + 2 + jnp.where(late, jnp.maximum(0, N - 6 * behind // 2), 0)

    t_before = jnp.where(zpos >= 4, 0, N)
    t_after = jnp.where(late, l_b, l_b + N)

    def slot(t, carry):
        @pl.when(t == t_before)
        def _():
            pl.loop(0, HEADS)(before)

        one.slot(t)
        i = t - l_g1


        @pl.when((i >= 0) & (i < N))
        def _():
            one.finish(i)

            @pl.when((i > 0) & (lax.rem(i, PER_HEAD) == 0))
            def _():
                middle(i // PER_HEAD - 1)
                after(i // PER_HEAD - 1)

        two.slot(t - l_b)
        k = t - l_g2

        @pl.when((k >= 0) & (k < N))
        def _():
            two.finish(k)

            @pl.when((k < N - 1) & (lax.rem(k + 1, PER_HEAD) == 0))
            def _():
                last(k // PER_HEAD)

        return carry

    lax.fori_loop(0, N + l_g2, slot, 0)

    @pl.loop(0, HEADS)
    def _(h):
        c = cols(h)
        kg_ref[:, c] = ((ki_ref[:, c] + p2[N - 1, pl.ds(h, 1), :]) * slope(k_ref[:, c])).astype(BF16)

    one.drain()
    two.drain()


def per_device(queries, keys, values, cotangent):
    wide = HEADS * HD
    single = pltpu.VMEM((N, CHUNK, HD), F32)
    double = pltpu.VMEM((N, 2, CHUNK, HD), F32)
    bufs = [single, double, double] + [single] * (N_BUFS - 3)
    low = pltpu.VMEM((TOK, wide), BF16)
    full = pltpu.VMEM((TOK, wide), F32)
    thin = pltpu.VMEM((HEADS, TOK, 1), F32)
    sems = [pltpu.SemaphoreType.DMA((7, N)), pltpu.SemaphoreType.DMA((7,))]
    vmem = pl.BlockSpec(memory_space=pltpu.VMEM)
    return pl.pallas_call(
        kernel,
        out_shape=[jax.ShapeDtypeStruct((TOK, wide), BF16)] * 4,
        in_specs=[vmem] * 4,
        out_specs=[vmem] * 4,
        scratch_shapes=[low, low, full, full, low, low, thin, thin] + [single] * 4 + bufs * 2 + sems * 2,
        compiler_params=pltpu.CompilerParams(collective_id=0, has_side_effects=True, vmem_limit_bytes=63 << 20),
        name="linear_attention",
    )(queries, keys, values, cotangent)


def solution(mesh):
    spec = P(("outer", "inner"), None)
    return jax.shard_map(per_device, mesh=mesh, in_specs=(spec,) * 4, out_specs=(spec,) * 4, check_vma=False)
```
